32 devices in a mesh: rows: 8 (over z, y), cols: 4 (over x, core).
Axes of the slice: x: 2, y: 2, z: 4, core: 2. Of those that a mesh axis runs over, the one named last changes fastest.
Arguments:
- genotypes: int32 [5120, 2048], P('rows', 'cols'), may hold values from 0 to 2
- frequencies: float32 [2048], P('cols'), may hold values from 0.05 to 0.5
- traits: bfloat16 [5120, 32768], P('rows', 'cols'), may hold values from -6 to 6
- geno_sketch: bfloat16 [2048, 512], P('cols'), may hold values from -0.125 to 0.125
- trait_sketch: bfloat16 [32768, 512], P('cols'), may hold values from -0.03125 to 0.03125
- initial: float32 [512, 256], replicated, may hold values from -6 to 6
Outputs:
- geno_scores: bfloat16 [5120, 256], P('rows')
- trait_scores: bfloat16 [5120, 256], P('rows')
- geno_loadings: float32 [256, 2048], P('rows', 'cols')
- trait_loadings: float32 [256, 32768], P('rows', 'cols')
The draws below stay inside these ranges and needn't reach their ends.
All inputs are finite; a program needn't handle non-finite values.
Results may differ from the reference program's by a relative error of at most 0.0059.
Values sent between devices are 32-bit elements; how exact they have to be, the bound alone decides.
No kernel may reach another device: no remote copies, remote signals or barrier semaphores. Data moves between devices by JAX's collectives and lax.ppermute only.
A program may use at most 128 MiB of HBM per device.

```python
import math
import jax
import jax.numpy as jnp
from jax import lax

TRAITS = 32768
SKETCH = 512
PAIRS = 256
PEOPLE = 5120
GENO = 2048


def plant(array, key, least, top_value):
    longest = array.shape.index(max(array.shape))
    spots = []
    for shift in (0, 1):
        where = [jax.random.randint(jax.random.fold_in(key, axis), (), 0, length) for axis, length in enumerate(array.shape)]
        where[longest] = (where[longest] + shift) % array.shape[longest]
        spots.append(tuple(where))
    return array.at[spots[0]].set(least).at[spots[1]].set(top_value)


def shard_levels(own_key, extent, pieces, smallest, high):
    factor_of, own = 1.0, jax.random.fold_in(own_key, 6)
    for dim, shards_of in pieces:
        steps = jnp.exp(jax.random.uniform(jax.random.fold_in(own, dim), (shards_of,), jnp.float32, smallest / len(pieces), high / len(pieces)))
        factor_of = factor_of * jnp.repeat(steps, extent[dim] // shards_of).reshape([-1 if axis == dim else 1 for axis in range(len(extent))])
    return factor_of


def centred(own_key, dims, deviation, reach, cuts=(), kind=jnp.bfloat16):
    loudness = shard_levels(own_key, dims, cuts, -0.22, 0.18) if cuts else 1.0
    values = jax.random.normal(own_key, dims, jnp.float32) * deviation * loudness
    return jnp.minimum(jnp.maximum(values, -reach), reach).astype(kind)


def setup_inputs(seed: int = 0) -> dict:
    arg_keys = jax.random.split(jax.random.key(seed), 7)
    genotypes = plant(jax.random.randint(arg_keys[0], (PEOPLE, GENO), 0, 3), jax.random.fold_in(arg_keys[0], 1), 0, 2).astype(jnp.int32)
    frequencies = jnp.clip(jnp.exp(math.log(0.5) - 2.3025851 * jax.random.uniform(arg_keys[1], (GENO,), jnp.float32) ** shard_levels(arg_keys[1], (GENO,), ((0, 4),), -0.2, 0.2)), 0.05, 0.5)
    traits = centred(arg_keys[2], (PEOPLE, TRAITS), 1.0, 6.0, ((0, 8), (1, 4)))
    geno_sketch = centred(arg_keys[3], (GENO, SKETCH), GENO ** -0.5, 0.125, ((0, 4),))
    trait_sketch = centred(arg_keys[4], (TRAITS, SKETCH), TRAITS ** -0.5, 0.03125, ((0, 4),))
    initial = centred(arg_keys[5], (SKETCH, PAIRS), 1.0, 6.0, (), jnp.float32)
    return {"genotypes": genotypes, "frequencies": frequencies, "traits": traits, "geno_sketch": geno_sketch, "trait_sketch": trait_sketch, "initial": initial}


def standard(genotypes, frequencies):
    spread = lax.rsqrt(2.0 * frequencies * (1.0 - frequencies))
    return ((genotypes.astype(jnp.float32) - 2.0 * frequencies) * spread).astype(jnp.bfloat16)

def unit_columns(matrix):
    return matrix * lax.rsqrt(lax.optimization_barrier(jnp.mean(matrix * matrix, axis=0, keepdims=True)) + 1e-06)

def make_basis(sketch_view):
    gram_view = jnp.dot(sketch_view.T, sketch_view, precision=lax.Precision.HIGHEST) / PEOPLE
    lower_view = jnp.linalg.cholesky(gram_view)
    return lax.linalg.triangular_solve(lower_view, sketch_view, left_side=False, lower=True, transpose_a=True)

def reference(genotypes, frequencies, traits, geno_sketch, trait_sketch, initial):
    standardized = standard(genotypes, frequencies)
    sketch_geno = jnp.dot(standardized.astype(jnp.float32), geno_sketch.astype(jnp.float32), preferred_element_type=jnp.float32)
    sketch_trait = jnp.dot(traits.astype(jnp.float32), trait_sketch.astype(jnp.float32), preferred_element_type=jnp.float32)
    basis_geno = make_basis(sketch_geno)
    basis_trait = make_basis(sketch_trait)
    crossed = jnp.dot(basis_geno.T, basis_trait, precision=lax.Precision.HIGHEST) / PEOPLE
    left_dirs = unit_columns(jnp.dot(crossed, initial, precision=lax.Precision.HIGHEST))
    right_dirs = unit_columns(jnp.dot(crossed.T, left_dirs, precision=lax.Precision.HIGHEST))
    root_sketch = math.sqrt(SKETCH)
    geno_scores = (jnp.dot(basis_geno, left_dirs, precision=lax.Precision.HIGHEST) / root_sketch).astype(jnp.bfloat16)
    trait_scores = (jnp.dot(basis_trait, right_dirs, precision=lax.Precision.HIGHEST) / root_sketch).astype(jnp.bfloat16)
    root_people = math.sqrt(PEOPLE)
    geno_loadings = jnp.dot(geno_scores.T.astype(jnp.float32), standardized.astype(jnp.float32), preferred_element_type=jnp.float32) / root_people
    trait_loadings = jnp.dot(trait_scores.T.astype(jnp.float32), traits.astype(jnp.float32), preferred_element_type=jnp.float32) / root_people
    return (geno_scores, trait_scores, geno_loadings, trait_loadings)
```

```python
import functools
import math

import jax
import jax.numpy as jnp
from jax import lax
from jax.experimental import pallas as pl
from jax.experimental.pallas import tpu as pltpu
from jax.sharding import PartitionSpec as P

EXACT = lax.Precision.HIGHEST


def eliminate(block, out_ref):
    size = block.shape[0]
    lanes = lax.broadcasted_iota(jnp.int32, (8, size), 1)
    subs = lax.broadcasted_iota(jnp.int32, (8, size), 0)
    groups = [block[8 * g : 8 * g + 8, :] for g in range(size // 8)]
    for j in range(size):
        own, s = divmod(j, 8)
        row = groups[own][s : s + 1, :]
        pivot = row[:, j : j + 1]
        unit_row = jnp.where(lanes[:1] == j, 1.0, row)
        scaled = unit_row * (1.0 / pivot)
        for g in range(own, size // 8):
            if g == own and s == 7:
                continue
            here = groups[g]
            col = here[:, j : j + 1]
            fresh = jnp.where(lanes == j, 0.0, here) - col * scaled
            groups[g] = fresh if g > own else jnp.where(subs > s, fresh, here)
        out_ref[j : j + 1, :] = jnp.where(lanes[:1] <= j, unit_row, 0.0) * lax.rsqrt(pivot)


def factor_kernel(gram_ref, inv_ref, small_ref, *, width):
    n = gram_ref.shape[0]
    inv_ref[...] = gram_ref[...]
    rows = lax.broadcasted_iota(jnp.int32, (1, n), 1)
    wide = lax.broadcasted_iota(jnp.int32, (width, n), 1)
    deep = lax.broadcasted_iota(jnp.int32, (width, n), 0)
    def step(k, carry):
        at = pl.multiple_of(k * width, width)
        eliminate(inv_ref[pl.ds(at, width), pl.ds(at, width)], small_ref)
        panel = inv_ref[pl.ds(at, width), :]
        inside = (wide >= at) & (wide < at + width)
        panel = jnp.where(inside, jnp.where(wide - at == deep, 1.0, 0.0), panel)
        panel = jnp.dot(small_ref[...], panel, precision=EXACT, preferred_element_type=jnp.float32)
        below = jnp.where(wide >= at + width, panel, 0.0)
        update = lax.dot_general(below, panel, (((0,), (0,)), ((), ())), precision=EXACT, preferred_element_type=jnp.float32)
        for i in range(n // width):
            old = inv_ref[i * width : (i + 1) * width, :]
            old = jnp.where(inside & (i > k), 0.0, old)
            inv_ref[i * width : (i + 1) * width, :] = old - update[i * width : (i + 1) * width, :]
        inv_ref[pl.ds(at, width), :] = jnp.where(wide < at + width, panel, 0.0)
        return carry
    lax.fori_loop(0, n // width, step, 0)


def inverse_factor(gram):
    size = gram.shape[0]
    width = math.gcd(size, 128)
    return pl.pallas_call(
        functools.partial(factor_kernel, width=width),
        out_shape=jax.ShapeDtypeStruct((size, size), jnp.float32),
        in_specs=[pl.BlockSpec(memory_space=pltpu.VMEM)],
        out_specs=pl.BlockSpec(memory_space=pltpu.VMEM),
        scratch_shapes=[pltpu.VMEM((width, width), jnp.float32)],
        name="inverse_factor",
    )(gram)


def standard(genotypes, frequencies):
    spread = lax.rsqrt(2.0 * frequencies * (1.0 - frequencies))
    return ((genotypes.astype(jnp.float32) - 2.0 * frequencies) * spread).astype(jnp.bfloat16)


def unit_columns(matrix):
    return matrix * lax.rsqrt(jnp.mean(matrix * matrix, axis=0, keepdims=True) + 1e-06)


def exact_dot(left_side, right_side, contract):
    return lax.dot_general(
        left_side,
        right_side,
        ((contract[:1], contract[1:]), ((), ())),
        precision=EXACT,
        preferred_element_type=jnp.float32,
    )


def masks_of(size):
    return [1 << bit for bit in range(size.bit_length() - 1)]


def swap(value, axis, mask):
    size = lax.axis_size(axis)
    return lax.ppermute(value, axis, [(i, i ^ mask) for i in range(size)])


def side_of(axis, mask):
    return jnp.minimum(lax.axis_index(axis) & mask, 1)


def halve(value, axis, mask):
    half = value.shape[0] // 2
    side = side_of(axis, mask)
    kept = lax.dynamic_slice_in_dim(value, side * half, half)
    sent = lax.dynamic_slice_in_dim(value, (1 - side) * half, half)
    return kept + swap(sent, axis, mask)


def double(value, axis, mask):
    side = side_of(axis, mask)
    half = value.shape[0]
    whole = jnp.concatenate([value, value], axis=0)
    return lax.dynamic_update_slice_in_dim(whole, swap(value, axis, mask), (1 - side) * half, 0)


def sum_over(value, axis, orders):
    part = value.shape[0] // len(orders)
    sums = []
    for at, masks in enumerate(orders):
        piece = value[at * part : (at + 1) * part]
        for mask in masks:
            piece = halve(piece, axis, mask)
        for mask in reversed(masks):
            piece = double(piece, axis, mask)
        sums.append(piece)
    return jnp.concatenate(sums, axis=0)


def ring_place(index, size):
    return jnp.where(index % 2 == 0, index // 2, size - (index + 1) // 2)


def ring_member(place, size):
    return jnp.where(2 * place < size, 2 * place, 2 * (size - place) - 1)


def ring_scatter(take, size, forward):
    members = [2 * q if 2 * q < size else 2 * (size - q) - 1 for q in range(size)]
    pairs = [(members[q], members[(q + 1) % size]) for q in range(size)]
    if not forward:
        pairs = [(b, a) for a, b in pairs]
    turn = 1 if forward else -1
    place = ring_place(lax.axis_index("rows"), size)
    total = take(ring_member((place - turn + size) % size, size))
    for step in range(size - 1):
        arrived = lax.ppermute(total, "rows", pairs)
        total = arrived + take(ring_member((place - turn * (step + 2) + 2 * size) % size, size))
    return total


def on_device(genotypes, frequencies, traits, geno_sketch, trait_sketch, initial):
    row_count, col_count = lax.axis_size("rows"), lax.axis_size("cols")
    people = genotypes.shape[0] * row_count
    sketch_width = geno_sketch.shape[1]
    col = lax.axis_index("cols")
    core, chip = col % 2, col // 2
    chips = col_count // 2
    wide_masks = masks_of(col_count)[1:]
    row_masks = masks_of(row_count)

    standardized = standard(genotypes, frequencies)

    def gathered(partial):
        part = halve(partial, "cols", 1)
        for mask in wide_masks:
            part = part + swap(part, "cols", mask)
        return double(part, "cols", 1)

    sketch_geno = gathered(jnp.dot(standardized, geno_sketch, preferred_element_type=jnp.float32))
    sketch_trait = gathered(jnp.dot(traits, trait_sketch, preferred_element_type=jnp.float32))

    own = jnp.where(core == 0, sketch_geno, sketch_trait)
    strip = sketch_width // chips
    own_strip = lax.dynamic_slice_in_dim(own, chip * strip, strip, 1)
    gram_part = exact_dot(own_strip, own, (0, 0))
    strip = sketch_width // col_count
    cross_strip = lax.dynamic_slice_in_dim(sketch_geno, (core * chips + chip) * strip, strip, 1)
    cross_part = exact_dot(cross_strip, sketch_trait, (0, 0))
    orders = (row_masks, row_masks[1:] + row_masks[:1])
    gram = sum_over(gram_part, "rows", orders)
    cross = sum_over(cross_part, "rows", orders)
    for mask in wide_masks:
        gram = double(gram, "cols", mask)
        cross = double(cross, "cols", mask)
    cross = double(cross, "cols", 1)

    own_inverse = inverse_factor(gram / people)
    other_inverse = swap(own_inverse, "cols", 1)
    inverse_geno = jnp.where(core == 0, own_inverse, other_inverse)
    inverse_trait = jnp.where(core == 0, other_inverse, own_inverse)

    moved = exact_dot(cross, exact_dot(inverse_trait, initial, (0, 0)), (1, 0)) / people
    left_dirs = unit_columns(exact_dot(inverse_geno, moved, (1, 0)))
    geno_weights = exact_dot(inverse_geno, left_dirs, (0, 0))
    moved = exact_dot(cross, geno_weights, (0, 0)) / people
    right_dirs = unit_columns(exact_dot(inverse_trait, moved, (1, 0)))
    trait_weights = exact_dot(inverse_trait, right_dirs, (0, 0))

    root_sketch = math.sqrt(sketch_width)
    geno_scores = (exact_dot(sketch_geno, geno_weights, (1, 0)) / root_sketch).astype(jnp.bfloat16)
    trait_scores = (exact_dot(sketch_trait, trait_weights, (1, 0)) / root_sketch).astype(jnp.bfloat16)

    def term(scores, block):
        return lax.dot_general(scores, block, (((0,), (0,)), ((), ())), preferred_element_type=jnp.float32)

    pairs = geno_scores.shape[1]
    share = pairs // row_count
    streams = 4
    geno_share, trait_share = standardized.shape[1] // streams, traits.shape[1] // streams
    geno_term = term(geno_scores, standardized)
    summed = []
    for at in range(streams):
        trait_term = term(trait_scores, traits[:, at * trait_share : (at + 1) * trait_share])
        geno_piece = geno_term[:, at * geno_share : (at + 1) * geno_share]

        def take(member, geno_piece=geno_piece, trait_term=trait_term):
            return jnp.concatenate(
                [lax.dynamic_slice_in_dim(piece, member * share, share) for piece in (geno_piece, trait_term)],
                axis=1,
            )

        summed.append(ring_scatter(take, row_count, at % 2 == 0))
    root_people = math.sqrt(people)
    geno_loadings = jnp.concatenate([piece[:, :geno_share] for piece in summed], axis=1) / root_people
    trait_loadings = jnp.concatenate([piece[:, geno_share:] for piece in summed], axis=1) / root_people
    return (geno_scores, trait_scores, geno_loadings, trait_loadings)


def solution(mesh):
    placed = (
        P("rows", "cols"),
        P("cols"),
        P("rows", "cols"),
        P("cols", None),
        P("cols", None),
        P(),
    )
    return jax.shard_map(
        on_device,
        mesh=mesh,
        in_specs=placed,
        out_specs=(P("rows", None), P("rows", None), P("rows", "cols"), P("rows", "cols")),
        check_vma=False,
    )
```

```python
import functools
import math

import jax
import jax.numpy as jnp
from jax import lax
from jax.experimental import pallas as pl
from jax.experimental.pallas import tpu as pltpu
from jax.sharding import PartitionSpec as P

EXACT = lax.Precision.HIGHEST
CLOSE = lax.Precision.HIGH


def eliminate(block, out_ref, tall=8):
    size = block.shape[0]
    shape = (8, size)
    lanes = lax.broadcasted_iota(jnp.int32, shape, 1)
    subs = lax.broadcasted_iota(jnp.int32, shape, 0)
    groups = [block[8 * g : 8 * g + 8, :] for g in range(size // 8)]
    for first in range(0, size, tall):
        own, s = divmod(first, 8)
        here = groups[own]
        spread = [jnp.broadcast_to(here[:, first + k : first + k + 1], shape) for k in range(tall)]
        a = [[jnp.broadcast_to(spread[k][s + i : s + i + 1, :], shape) for k in range(i + 1)] for i in range(tall)]
        inside = (lanes >= first) & (lanes < first + tall)
        unit = jnp.where(inside, jnp.where(lanes - first == subs - s, 1.0, 0.0), here)
        rows = [jnp.broadcast_to(unit[s + k : s + k + 1, :], shape) for k in range(tall)]
        inverse, lower = [], {}
        for i in range(tall):
            inverse.append(1.0 / a[i][i])
            for k in range(i + 1, tall):
                lower[k, i] = a[k][i] * inverse[i]
                for m in range(i + 1, k + 1):
                    a[k][m] = a[k][m] - lower[k, i] * a[m][i]
                rows[k] = rows[k] - lower[k, i] * rows[i]
        final = rows[0] * lax.rsqrt(a[0][0])
        for i in range(1, tall):
            final = jnp.where(subs == s + i, rows[i] * lax.rsqrt(a[i][i]), final)
        out_ref[first : first + tall, :] = jnp.where(lanes <= 8 * own + subs, final, 0.0)[s : s + tall, :]
        back = [None] * tall
        for k in reversed(range(tall)):
            back[k] = rows[k] * inverse[k]
            for i in range(k + 1, tall):
                back[k] = back[k] - lower[i, k] * back[i]
        for g in range(own if s + tall < 8 else own + 1, size // 8):
            old = groups[g]
            fresh = jnp.where(inside, 0.0, old)
            for k in range(tall):
                col = spread[k] if g == own else jnp.broadcast_to(old[:, first + k : first + k + 1], shape)
                fresh = fresh - col * back[k]
            groups[g] = fresh if g > own else jnp.where(subs >= s + tall, fresh, old)


def factor_in_place(ref, small_ref):
    n, width = ref.shape[0], small_ref.shape[0]
    wide = lax.broadcasted_iota(jnp.int32, (width, n), 1)
    deep = lax.broadcasted_iota(jnp.int32, (width, n), 0)

    def step(k, carry):
        at = pl.multiple_of(k * width, width)
        eliminate(ref[pl.ds(at, width), pl.ds(at, width)], small_ref)
        panel = ref[pl.ds(at, width), :]
        inside = (wide >= at) & (wide < at + width)
        panel = jnp.where(inside, jnp.where(wide - at == deep, 1.0, 0.0), panel)
        panel = jnp.dot(small_ref[...], panel, precision=EXACT, preferred_element_type=jnp.float32)
        below = jnp.where(wide >= at + width, panel, 0.0)
        update = lax.dot_general(
            below, panel, (((0,), (0,)), ((), ())), precision=EXACT, preferred_element_type=jnp.float32
        )
        for i in range(n // width):
            old = ref[i * width : (i + 1) * width, :]
            old = jnp.where(inside & (i > k), 0.0, old)
            ref[i * width : (i + 1) * width, :] = old - update[i * width : (i + 1) * width, :]
        ref[pl.ds(at, width), :] = jnp.where(wide < at + width, panel, 0.0)
        return carry

    lax.fori_loop(0, n // width, step, 0)


def factor_whole_kernel(gram_ref, inverse_ref, small_ref, *, scale):
    inverse_ref[...] = gram_ref[...] * scale
    factor_in_place(inverse_ref, small_ref)


def factor_pieces_kernel(place_ref, *refs, scale):
    piece_refs, (inverse_ref, small_ref, held_ref) = refs[:4], refs[4:]
    half = inverse_ref.shape[0] // 2
    rows = half // 2
    for at, piece_ref in enumerate(piece_refs):
        chip, side = place_ref[0] ^ (at // 2), place_ref[1] ^ (at % 2)
        held_ref[chip, pl.ds(pl.multiple_of(side * rows, rows), rows), :] = piece_ref[...] * scale
    inverse_ref[:half, :half] = held_ref[0, :, :half]
    inverse_ref[:half, half : half + rows] = held_ref[0, :, half:]
    inverse_ref[:half, half + rows :] = held_ref[1, :, half:]
    inverse_ref[half:, :half] = jnp.zeros((half, half), jnp.float32)
    inverse_ref[half:, half:] = held_ref[1, :, :half]
    factor_in_place(inverse_ref, small_ref)


def inverse_factor(pieces, place, size, scale):
    width = math.gcd(size, 128)
    vmem = pl.BlockSpec(memory_space=pltpu.VMEM)
    scratch = [pltpu.VMEM((width, width), jnp.float32)]
    if place is None:
        kernel, specs = factor_whole_kernel, [vmem]
    else:
        kernel, specs = factor_pieces_kernel, [pl.BlockSpec(memory_space=pltpu.SMEM)] + [vmem] * 4
        scratch.append(pltpu.VMEM((2, size // 2, size // 4 * 3), jnp.float32))
        pieces = (place, *pieces)
    return pl.pallas_call(
        functools.partial(kernel, scale=scale),
        out_shape=jax.ShapeDtypeStruct((size, size), jnp.float32),
        in_specs=specs,
        out_specs=vmem,
        scratch_shapes=scratch,
        name="inverse_factor",
    )(*pieces)


def standard(genotypes, frequencies):
    spread = lax.rsqrt(2.0 * frequencies * (1.0 - frequencies))
    return ((genotypes.astype(jnp.float32) - 2.0 * frequencies) * spread).astype(jnp.bfloat16)


def unit_columns(matrix):
    return matrix * lax.rsqrt(jnp.mean(matrix * matrix, axis=0, keepdims=True) + 1e-06)


def dot(left_side, right_side, contract, precision):
    return lax.dot_general(
        left_side,
        right_side,
        ((contract[:1], contract[1:]), ((), ())),
        precision=precision,
        preferred_element_type=jnp.float32,
    )


def masks_of(size):
    return [1 << bit for bit in range(size.bit_length() - 1)]


def swap(value, axis, mask):
    size = lax.axis_size(axis)
    return lax.ppermute(value, axis, [(i, i ^ mask) for i in range(size)])


def side_of(axis, mask):
    return jnp.minimum(lax.axis_index(axis) & mask, 1)


def halve(value, axis, mask):
    half = value.shape[0] // 2
    side = side_of(axis, mask)
    kept = lax.dynamic_slice_in_dim(value, side * half, half)
    sent = lax.dynamic_slice_in_dim(value, (1 - side) * half, half)
    return kept + swap(sent, axis, mask)


def double(value, axis, mask):
    side = side_of(axis, mask)
    half = value.shape[0]
    whole = jnp.concatenate([value, value], axis=0)
    return lax.dynamic_update_slice_in_dim(whole, swap(value, axis, mask), (1 - side) * half, 0)


def ring_place(index, size):
    return jnp.where(index % 2 == 0, index // 2, size - (index + 1) // 2)


def ring_member(place, size):
    return jnp.where(2 * place < size, 2 * place, 2 * (size - place) - 1)


def ring_scatter(take, size, forward):
    members = [2 * q if 2 * q < size else 2 * (size - q) - 1 for q in range(size)]
    pairs = [(members[q], members[(q + 1) % size]) for q in range(size)]
    if not forward:
        pairs = [(b, a) for a, b in pairs]
    turn = 1 if forward else -1
    place = ring_place(lax.axis_index("rows"), size)
    total = take(ring_member((place - turn + size) % size, size))
    for step in range(size - 1):
        arrived = lax.ppermute(total, "rows", pairs)
        total = arrived + take(ring_member((place - turn * (step + 2) + 2 * size) % size, size))
    return total


def sum_rows(value, masks):
    for mask in masks[:-1]:
        value = halve(value, "rows", mask)
    value = value + swap(value, "rows", masks[-1])
    for mask in reversed(masks[1:-1]):
        value = double(value, "rows", mask)
    return value


def on_device(genotypes, frequencies, traits, geno_sketch, trait_sketch, initial):
    row_count, col_count = lax.axis_size("rows"), lax.axis_size("cols")
    people = genotypes.shape[0] * row_count
    size = geno_sketch.shape[1]
    col = lax.axis_index("cols")
    core, chip = col % 2, col // 2
    chips = col_count // 2
    wide_masks = masks_of(col_count)[1:]
    row_masks = masks_of(row_count)

    standardized = standard(genotypes, frequencies)

    def over_chips(part):
        for mask in wide_masks:
            moved = swap(part, "cols", mask)
            part = part + moved
        return part

    partial_geno = jnp.dot(standardized, geno_sketch, preferred_element_type=jnp.float32)
    chip_geno = halve(partial_geno, "cols", 1)
    height = genotypes.shape[0] // 2
    late_traits, chip_geno = lax.optimization_barrier((traits, chip_geno))
    partial_trait = jnp.dot(late_traits, trait_sketch, preferred_element_type=jnp.float32)
    half_geno = over_chips(chip_geno)
    half_trait = over_chips(halve(partial_trait, "cols", 1))

    mine = jnp.where(core == 0, half_geno, half_trait)
    others = jnp.where(core == 0, half_trait, half_geno)
    arrived = swap(others, "cols", 1)

    def gram_of(left_of, right_of):
        return sum(dot(left_of(view), right_of(view), (0, 0), EXACT) for view in (mine, arrived))

    def columns(at, width):
        return lambda view: lax.dynamic_slice_in_dim(view, at, width, 1)

    if chips == 2:
        half, quarter = size // 2, size // 4
        block = gram_of(columns(chip * half, half), columns(chip * half, half))
        side = gram_of(columns(0, half), columns(half + chip * quarter, quarter))
        gram = jnp.concatenate([block, side], axis=1)
    else:
        strip = size // chips
        gram = gram_of(columns(chip * strip, strip), lambda view: view)
    mine, others, arrived, gram = lax.optimization_barrier((mine, others, arrived, gram))
    gram = sum_rows(gram, row_masks)

    whole_mine = jnp.concatenate([mine, mine], axis=0)
    own = lax.dynamic_update_slice_in_dim(whole_mine, arrived, (1 - core) * height, 0)
    whole_others = jnp.concatenate([others, others], axis=0)
    other = lax.dynamic_update_slice_in_dim(whole_others, swap(mine, "cols", 1), (1 - core) * height, 0)
    sketch_geno = jnp.where(core == 0, own, other)
    sketch_trait = jnp.where(core == 0, other, own)

    strip = size // col_count
    cross_strip = lax.dynamic_slice_in_dim(sketch_geno, (core * chips + chip) * strip, strip, 1)
    cross = sum_rows(dot(cross_strip, sketch_trait, (0, 0), EXACT), row_masks)
    cross = double(cross, "rows", row_masks[0])
    for mask in wide_masks:
        cross = double(cross, "cols", mask)

    if chips == 2:
        beside = swap(gram, "rows", 1)
        across = swap(gram, "cols", 2)
        cells = [(r, c) for r in range(row_count) for c in range(col_count)]
        flat = [(r * col_count + c, (r ^ 1) * col_count + (c ^ 2)) for r, c in cells]
        corner = lax.ppermute(gram, ("rows", "cols"), flat)
        place = jnp.stack([chip, side_of("rows", 1)])
        own_inverse = inverse_factor((gram, beside, across, corner), place, size, 1.0 / people)
    else:
        gram = double(gram, "rows", row_masks[0])
        for mask in wide_masks:
            gram = double(gram, "cols", mask)
        own_inverse = inverse_factor((gram,), None, size, 1.0 / people)
    cross = double(cross, "cols", 1)
    other_inverse = swap(own_inverse, "cols", 1)
    inverse_geno = jnp.where(core == 0, own_inverse, other_inverse)
    inverse_trait = jnp.where(core == 0, other_inverse, own_inverse)

    moved = dot(cross, dot(inverse_trait, initial, (0, 0), CLOSE), (1, 0), CLOSE) / people
    left_dirs = unit_columns(dot(inverse_geno, moved, (1, 0), CLOSE))
    geno_weights = dot(inverse_geno, left_dirs, (0, 0), CLOSE)
    moved = dot(cross, geno_weights, (0, 0), CLOSE) / people
    right_dirs = unit_columns(dot(inverse_trait, moved, (1, 0), CLOSE))
    trait_weights = dot(inverse_trait, right_dirs, (0, 0), CLOSE)

    root_size = math.sqrt(size)
    geno_scores = (dot(sketch_geno, geno_weights, (1, 0), CLOSE) / root_size).astype(jnp.bfloat16)
    trait_scores = (dot(sketch_trait, trait_weights, (1, 0), CLOSE) / root_size).astype(jnp.bfloat16)

    def term(scores, block):
        return lax.dot_general(scores, block, (((0,), (0,)), ((), ())), preferred_element_type=jnp.float32)

    pairs = geno_scores.shape[1]
    share = pairs // row_count
    streams = 4
    geno_share, trait_share = standardized.shape[1] // streams, traits.shape[1] // streams
    geno_term = term(geno_scores, standardized)
    summed = []
    for at in range(streams):
        trait_term = term(trait_scores, traits[:, at * trait_share : (at + 1) * trait_share])
        geno_piece = geno_term[:, at * geno_share : (at + 1) * geno_share]

        def take(member, geno_piece=geno_piece, trait_term=trait_term):
            return jnp.concatenate(
                [lax.dynamic_slice_in_dim(piece, member * share, share) for piece in (geno_piece, trait_term)],
                axis=1,
            )

        summed.append(ring_scatter(take, row_count, at % 2 == 0))
    root_people = math.sqrt(people)
    geno_loadings = jnp.concatenate([piece[:, :geno_share] for piece in summed], axis=1) / root_people
    trait_loadings = jnp.concatenate([piece[:, geno_share:] for piece in summed], axis=1) / root_people
    return (geno_scores, trait_scores, geno_loadings, trait_loadings)


def solution(mesh):
    placed = (
        P("rows", "cols"),
        P("cols"),
        P("rows", "cols"),
        P("cols", None),
        P("cols", None),
        P(),
    )
    return jax.shard_map(
        on_device,
        mesh=mesh,
        in_specs=placed,
        out_specs=(P("rows", None), P("rows", None), P("rows", "cols"), P("rows", "cols")),
        check_vma=False,
    )
```

```python
import functools
import math

import jax
import jax.numpy as jnp
from jax import lax
from jax.experimental import pallas as pl
from jax.experimental.pallas import tpu as pltpu
from jax.sharding import PartitionSpec as P

EXACT = lax.Precision.HIGHEST
CLOSE = lax.Precision.HIGH
ROUNDS = 3


def eliminate(block, out_ref, tall=8):
    size = block.shape[0]
    shape = (8, size)
    lanes = lax.broadcasted_iota(jnp.int32, shape, 1)
    subs = lax.broadcasted_iota(jnp.int32, shape, 0)
    groups = [block[8 * g : 8 * g + 8, :] for g in range(size // 8)]
    for first in range(0, size, tall):
        own, s = divmod(first, 8)
        here = groups[own]
        spread = [jnp.broadcast_to(here[:, first + k : first + k + 1], shape) for k in range(tall)]
        a = [[jnp.broadcast_to(spread[k][s + i : s + i + 1, :], shape) for k in range(i + 1)] for i in range(tall)]
        inside = (lanes >= first) & (lanes < first + tall)
        unit = jnp.where(inside, jnp.where(lanes - first == subs - s, 1.0, 0.0), here)
        rows = [jnp.broadcast_to(unit[s + k : s + k + 1, :], shape) for k in range(tall)]
        inverse, lower = [None] * tall, {}
        for i in range(0, tall, 2):
            p, q, r = a[i][i], a[i + 1][i], a[i + 1][i + 1]
            both = p * r - q * q
            inverse[i] = 1.0 / p
            lower[i + 1, i] = q * inverse[i]
            inverse[i + 1] = p * (1.0 / both)
            a[i + 1][i + 1] = r - lower[i + 1, i] * q
            rows[i + 1] = rows[i + 1] - lower[i + 1, i] * rows[i]
            for k in range(i + 2, tall):
                lower[k, i] = a[k][i] * inverse[i]
                a[k][i + 1] = a[k][i + 1] - lower[k, i] * q
                lower[k, i + 1] = a[k][i + 1] * inverse[i + 1]
                for m in range(i + 2, k + 1):
                    a[k][m] = a[k][m] - lower[k, i] * a[m][i] - lower[k, i + 1] * a[m][i + 1]
                rows[k] = rows[k] - lower[k, i] * rows[i] - lower[k, i + 1] * rows[i + 1]
        final = rows[0] * lax.rsqrt(a[0][0])
        for i in range(1, tall):
            final = jnp.where(subs == s + i, rows[i] * lax.rsqrt(a[i][i]), final)
        out_ref[first : first + tall, :] = jnp.where(lanes <= 8 * own + subs, final, 0.0)[s : s + tall, :]
        back = [None] * tall
        for k in reversed(range(tall)):
            back[k] = rows[k] * inverse[k]
            for i in range(k + 1, tall):
                back[k] = back[k] - lower[i, k] * back[i]
        for g in range(own if s + tall < 8 else own + 1, size // 8):
            old = groups[g]
            fresh = jnp.where(inside, 0.0, old)
            for k in range(tall):
                col = spread[k] if g == own else jnp.broadcast_to(old[:, first + k : first + k + 1], shape)
                fresh = fresh - col * back[k]
            groups[g] = fresh if g > own else jnp.where(subs >= s + tall, fresh, old)


def factor_in_place(ref, small_ref, panel_ref):
    n, width = ref.shape[0], small_ref.shape[0]
    wide = lax.broadcasted_iota(jnp.int32, (width, n), 1)
    deep = lax.broadcasted_iota(jnp.int32, (width, n), 0)

    def step(k, carry):
        at = pl.multiple_of(k * width, width)
        eliminate(ref[pl.ds(at, width), pl.ds(at, width)], small_ref)
        panel = ref[pl.ds(at, width), :]
        inside = (wide >= at) & (wide < at + width)
        panel = jnp.where(inside, jnp.where(wide - at == deep, 1.0, 0.0), panel)
        panel = jnp.dot(small_ref[...], panel, precision=EXACT, preferred_element_type=jnp.float32)
        panel_ref[...] = panel
        ref[pl.ds(at, width), :] = jnp.where(wide < at + width, panel, 0.0)

        def lower_rows(i, carry):
            spot = pl.multiple_of(i * width, width)
            change = lax.dot_general(
                panel_ref[:, pl.ds(spot, width)],
                panel,
                (((0,), (0,)), ((), ())),
                precision=EXACT,
                preferred_element_type=jnp.float32,
            )
            ref[pl.ds(spot, width), :] = jnp.where(inside, 0.0, ref[pl.ds(spot, width), :]) - change
            return carry

        lax.fori_loop(k + 1, n // width, lower_rows, 0)
        return carry

    lax.fori_loop(0, n // width, step, 0)


def factor_whole_kernel(gram_ref, inverse_ref, small_ref, panel_ref, *, scale):
    inverse_ref[...] = gram_ref[...] * scale
    factor_in_place(inverse_ref, small_ref, panel_ref)


def factor_pieces_kernel(place_ref, *refs, scale):
    piece_refs, (inverse_ref, small_ref, panel_ref, held_ref) = refs[:4], refs[4:]
    half = inverse_ref.shape[0] // 2
    rows = half // 2
    for at, piece_ref in enumerate(piece_refs):
        chip, side = place_ref[0] ^ (at // 2), place_ref[1] ^ (at % 2)
        held_ref[chip, pl.ds(pl.multiple_of(side * rows, rows), rows), :] = piece_ref[...] * scale
    inverse_ref[:half, :half] = held_ref[0, :, :half]
    inverse_ref[:half, half : half + rows] = held_ref[0, :, half:]
    inverse_ref[:half, half + rows :] = held_ref[1, :, half:]
    inverse_ref[half:, :half] = jnp.zeros((half, half), jnp.float32)
    inverse_ref[half:, half:] = held_ref[1, :, :half]
    factor_in_place(inverse_ref, small_ref, panel_ref)


def inverse_factor(pieces, place, size, scale):
    width = math.gcd(size, 128)
    vmem = pl.BlockSpec(memory_space=pltpu.VMEM)
    scratch = [pltpu.VMEM((width, width), jnp.float32), pltpu.VMEM((width, size), jnp.float32)]
    if place is None:
        kernel, specs = factor_whole_kernel, [vmem]
    else:
        kernel, specs = factor_pieces_kernel, [pl.BlockSpec(memory_space=pltpu.SMEM)] + [vmem] * 4
        scratch.append(pltpu.VMEM((2, size // 2, size // 4 * 3), jnp.float32))
        pieces = (place, *pieces)
    return pl.pallas_call(
        functools.partial(kernel, scale=scale),
        out_shape=jax.ShapeDtypeStruct((size, size), jnp.float32),
        in_specs=specs,
        out_specs=vmem,
        scratch_shapes=scratch,
        name="inverse_factor",
    )(*pieces)


def standard(genotypes, frequencies):
    spread = lax.rsqrt(2.0 * frequencies * (1.0 - frequencies))
    return ((genotypes.astype(jnp.float32) - 2.0 * frequencies) * spread).astype(jnp.bfloat16)


def unit_columns(matrix):
    return matrix * lax.rsqrt(jnp.mean(matrix * matrix, axis=0, keepdims=True) + 1e-06)


def dot(left_side, right_side, contract, precision):
    return lax.dot_general(
        left_side,
        right_side,
        ((contract[:1], contract[1:]), ((), ())),
        precision=precision,
        preferred_element_type=jnp.float32,
    )


def masks_of(size):
    return [1 << bit for bit in range(size.bit_length() - 1)]


def swap(value, axis, mask):
    size = lax.axis_size(axis)
    return lax.ppermute(value, axis, [(i, i ^ mask) for i in range(size)])


def side_of(axis, mask):
    return jnp.minimum(lax.axis_index(axis) & mask, 1)


def halve(value, axis, mask):
    half = value.shape[0] // 2
    side = side_of(axis, mask)
    kept = lax.dynamic_slice_in_dim(value, side * half, half)
    sent = lax.dynamic_slice_in_dim(value, (1 - side) * half, half)
    return kept + swap(sent, axis, mask)


def double(value, axis, mask):
    side = side_of(axis, mask)
    half = value.shape[0]
    whole = jnp.concatenate([value, value], axis=0)
    return lax.dynamic_update_slice_in_dim(whole, swap(value, axis, mask), (1 - side) * half, 0)


def ring_place(index, size):
    return jnp.where(index % 2 == 0, index // 2, size - (index + 1) // 2)


def ring_member(place, size):
    return jnp.where(2 * place < size, 2 * place, 2 * (size - place) - 1)


def ring_scatter(take, size, forward):
    members = [2 * q if 2 * q < size else 2 * (size - q) - 1 for q in range(size)]
    pairs = [(members[q], members[(q + 1) % size]) for q in range(size)]
    if not forward:
        pairs = [(b, a) for a, b in pairs]
    turn = 1 if forward else -1
    place = ring_place(lax.axis_index("rows"), size)
    total = take(ring_member((place - turn + size) % size, size))
    for step in range(size - 1):
        arrived = lax.ppermute(total, "rows", pairs)
        total = arrived + take(ring_member((place - turn * (step + 2) + 2 * size) % size, size))
    return total


def shares(geno_width, trait_width, rounds):
    tile = math.gcd(math.gcd(geno_width, trait_width), 256) // 2
    geno_half, trait_half = geno_width // 2, trait_width // 2
    first = max((geno_half + trait_half) // rounds // tile * tile - geno_half, tile)
    tiles = (trait_half - first) // tile
    ends = [first + tiles * at // max(rounds - 1, 1) * tile for at in range(rounds)]
    ends[-1] = trait_half
    spans = []
    for at in range(rounds):
        for way in range(2):
            start = ends[at - 1] if at else 0
            geno = (way * geno_half, (way + 1) * geno_half) if at == 0 else (0, 0)
            spans.append((geno, (way * trait_half + start, way * trait_half + ends[at])))
    return spans


def sum_rows(value, masks):
    for mask in masks[:-1]:
        value = halve(value, "rows", mask)
    moved = swap(value, "rows", masks[-1])
    value = value + moved
    for mask in reversed(masks[1:-1]):
        value = double(value, "rows", mask)
    return value


def whole_sum_rows(value, masks):
    moved = swap(value, "rows", masks[0])
    value = value + moved
    for mask in masks[1:-1]:
        value = halve(value, "rows", mask)
    moved = swap(value, "rows", masks[-1])
    value = value + moved
    for mask in reversed(masks[1:-1]):
        value = double(value, "rows", mask)
    return value


def on_device(genotypes, frequencies, traits, geno_sketch, trait_sketch, initial):
    row_count, col_count = lax.axis_size("rows"), lax.axis_size("cols")
    people = genotypes.shape[0] * row_count
    size = geno_sketch.shape[1]
    col = lax.axis_index("cols")
    core, chip = col % 2, col // 2
    chips = col_count // 2
    wide_masks = masks_of(col_count)[1:]
    row_masks = masks_of(row_count)

    standardized = standard(genotypes, frequencies)

    def over_chips(part):
        for mask in wide_masks:
            moved = swap(part, "cols", mask)
            part = part + moved
        return part

    partial_geno = jnp.dot(standardized, geno_sketch, preferred_element_type=jnp.float32)
    chip_geno = halve(partial_geno, "cols", 1)
    height = genotypes.shape[0] // 2
    late_traits, chip_geno = lax.optimization_barrier((traits, chip_geno))
    partial_trait = jnp.dot(late_traits, trait_sketch, preferred_element_type=jnp.float32)
    half_geno = over_chips(chip_geno)
    half_trait = over_chips(halve(partial_trait, "cols", 1))

    mine = jnp.where(core == 0, half_geno, half_trait)
    others = jnp.where(core == 0, half_trait, half_geno)
    arrived = swap(others, "cols", 1)

    def gram_of(left_of, right_of):
        return sum(dot(left_of(view), right_of(view), (0, 0), EXACT) for view in (mine, arrived))

    def columns(at, width):
        return lambda view: lax.dynamic_slice_in_dim(view, at, width, 1)

    if chips == 2:
        half, quarter = size // 2, size // 4
        block = gram_of(columns(chip * half, half), columns(chip * half, half))
        side = gram_of(columns(0, half), columns(half + chip * quarter, quarter))
        gram = jnp.concatenate([block, side], axis=1)
    else:
        strip = size // chips
        gram = gram_of(columns(chip * strip, strip), lambda view: view)
    mine, others, arrived, gram = lax.optimization_barrier((mine, others, arrived, gram))
    gram = sum_rows(gram, row_masks)

    whole_mine = jnp.concatenate([mine, mine], axis=0)
    own = lax.dynamic_update_slice_in_dim(whole_mine, arrived, (1 - core) * height, 0)
    whole_others = jnp.concatenate([others, others], axis=0)
    other = lax.dynamic_update_slice_in_dim(whole_others, swap(mine, "cols", 1), (1 - core) * height, 0)
    sketch_geno = jnp.where(core == 0, own, other)
    sketch_trait = jnp.where(core == 0, other, own)

    strip = size // col_count
    cross_strip = lax.dynamic_slice_in_dim(sketch_geno, col * strip, strip, 1)
    cross = whole_sum_rows(dot(cross_strip, sketch_trait, (0, 0), EXACT), row_masks)
    cross = double(cross, "cols", 1)
    for mask in wide_masks:
        cross = double(cross, "cols", mask)

    if chips == 2:
        beside = swap(gram, "rows", 1)
        across = swap(gram, "cols", 2)
        cells = [(r, c) for r in range(row_count) for c in range(col_count)]
        flat = [(r * col_count + c, (r ^ 1) * col_count + (c ^ 2)) for r, c in cells]
        corner = lax.ppermute(gram, ("rows", "cols"), flat)
        place = jnp.stack([chip, side_of("rows", 1)])
        own_inverse = inverse_factor((gram, beside, across, corner), place, size, 1.0 / people)
    else:
        gram = double(gram, "rows", row_masks[0])
        for mask in wide_masks:
            gram = double(gram, "cols", mask)
        own_inverse = inverse_factor((gram,), None, size, 1.0 / people)
    other_inverse = swap(own_inverse, "cols", 1)
    inverse_geno = jnp.where(core == 0, own_inverse, other_inverse)
    inverse_trait = jnp.where(core == 0, other_inverse, own_inverse)

    moved = dot(cross, dot(inverse_trait, initial, (0, 0), CLOSE), (1, 0), CLOSE) / people
    left_dirs = unit_columns(dot(inverse_geno, moved, (1, 0), CLOSE))
    geno_weights = dot(inverse_geno, left_dirs, (0, 0), CLOSE)
    moved = dot(cross, geno_weights, (0, 0), CLOSE) / people
    right_dirs = unit_columns(dot(inverse_trait, moved, (1, 0), CLOSE))
    trait_weights = dot(inverse_trait, right_dirs, (0, 0), CLOSE)

    root_size = math.sqrt(size)
    geno_scores = (dot(sketch_geno, geno_weights, (1, 0), CLOSE) / root_size).astype(jnp.bfloat16)
    trait_scores = (dot(sketch_trait, trait_weights, (1, 0), CLOSE) / root_size).astype(jnp.bfloat16)

    def term(scores, block):
        return lax.dot_general(scores, block, (((0,), (0,)), ((), ())), preferred_element_type=jnp.float32)

    pairs = geno_scores.shape[1]
    share = pairs // row_count
    spans = shares(standardized.shape[1], traits.shape[1], ROUNDS)
    geno_term = term(geno_scores, standardized)
    geno_sums, trait_sums = [], {}
    for at, (geno_span, trait_span) in enumerate(spans):
        trait_term = term(trait_scores, traits[:, slice(*trait_span)])
        edge = geno_span[1] - geno_span[0]
        pieces = [geno_term[:, slice(*geno_span)], trait_term] if edge else [trait_term]

        def take(member, pieces=pieces):
            parts = [lax.dynamic_slice_in_dim(piece, member * share, share) for piece in pieces]
            return jnp.concatenate(parts, axis=1) if len(parts) > 1 else parts[0]

        total = ring_scatter(take, row_count, at % 2 == 0)
        if edge:
            geno_sums.append(total[:, :edge])
        trait_sums[trait_span] = total[:, edge:]
    root_people = math.sqrt(people)
    geno_loadings = jnp.concatenate(geno_sums, axis=1) / root_people
    trait_loadings = jnp.concatenate([trait_sums[span] for span in sorted(trait_sums)], axis=1) / root_people
    return (geno_scores, trait_scores, geno_loadings, trait_loadings)


def solution(mesh):
    placed = (
        P("rows", "cols"),
        P("cols"),
        P("rows", "cols"),
        P("cols", None),
        P("cols", None),
        P(),
    )
    return jax.shard_map(
        on_device,
        mesh=mesh,
        in_specs=placed,
        out_specs=(P("rows", None), P("rows", None), P("rows", "cols"), P("rows", "cols")),
        check_vma=False,
    )
```

```python
import functools
import math

import jax
import jax.numpy as jnp
from jax import lax
from jax.experimental import pallas as pl
from jax.experimental.pallas import tpu as pltpu
from jax.sharding import PartitionSpec as P

EXACT = lax.Precision.HIGHEST
CLOSE = lax.Precision.HIGH
ROUNDS = 3


def eliminate(block, out_ref, tall=8):
    size = block.shape[0]
    shape = (8, size)
    lanes = lax.broadcasted_iota(jnp.int32, shape, 1)
    subs = lax.broadcasted_iota(jnp.int32, shape, 0)
    groups = [block[8 * g : 8 * g + 8, :] for g in range(size // 8)]
    for first in range(0, size, tall):
        own, s = divmod(first, 8)
        here = groups[own]
        spread = [jnp.broadcast_to(here[:, first + k : first + k + 1], shape) for k in range(tall)]
        a = [[jnp.broadcast_to(spread[k][s + i : s + i + 1, :], shape) for k in range(i + 1)] for i in range(tall)]
        inside = (lanes >= first) & (lanes < first + tall)
        unit = jnp.where(inside, jnp.where(lanes - first == subs - s, 1.0, 0.0), here)
        rows = [jnp.broadcast_to(unit[s + k : s + k + 1, :], shape) for k in range(tall)]
        inverse, lower = [None] * tall, {}
        for i in range(0, tall, 2):
            p, q, r = a[i][i], a[i + 1][i], a[i + 1][i + 1]
            both = p * r - q * q
            inverse[i] = 1.0 / p
            lower[i + 1, i] = q * inverse[i]
            inverse[i + 1] = p * (1.0 / both)
            a[i + 1][i + 1] = r - lower[i + 1, i] * q
            rows[i + 1] = rows[i + 1] - lower[i + 1, i] * rows[i]
            for k in range(i + 2, tall):
                lower[k, i] = a[k][i] * inverse[i]
                a[k][i + 1] = a[k][i + 1] - lower[k, i] * q
                lower[k, i + 1] = a[k][i + 1] * inverse[i + 1]
                for m in range(i + 2, k + 1):
                    a[k][m] = a[k][m] - lower[k, i] * a[m][i] - lower[k, i + 1] * a[m][i + 1]
                rows[k] = rows[k] - lower[k, i] * rows[i] - lower[k, i + 1] * rows[i + 1]
        final = rows[0] * lax.rsqrt(a[0][0])
        for i in range(1, tall):
            final = jnp.where(subs == s + i, rows[i] * lax.rsqrt(a[i][i]), final)
        out_ref[first : first + tall, :] = jnp.where(lanes <= 8 * own + subs, final, 0.0)[s : s + tall, :]
        back = [None] * tall
        for k in reversed(range(tall)):
            back[k] = rows[k] * inverse[k]
            for i in range(k + 1, tall):
                back[k] = back[k] - lower[i, k] * back[i]
        for g in range(own if s + tall < 8 else own + 1, size // 8):
            old = groups[g]
            fresh = jnp.where(inside, 0.0, old)
            for k in range(tall):
                col = spread[k] if g == own else jnp.broadcast_to(old[:, first + k : first + k + 1], shape)
                fresh = fresh - col * back[k]
            groups[g] = fresh if g > own else jnp.where(subs >= s + tall, fresh, old)


def factor_in_place(ref, small_ref, panel_ref):
    n, width = ref.shape[0], small_ref.shape[0]
    wide = lax.broadcasted_iota(jnp.int32, (width, n), 1)
    deep = lax.broadcasted_iota(jnp.int32, (width, n), 0)

    def step(k, carry):
        at = pl.multiple_of(k * width, width)
        eliminate(ref[pl.ds(at, width), pl.ds(at, width)], small_ref)
        panel = ref[pl.ds(at, width), :]
        inside = (wide >= at) & (wide < at + width)
        panel = jnp.where(inside, jnp.where(wide - at == deep, 1.0, 0.0), panel)
        panel = jnp.dot(small_ref[...], panel, precision=EXACT, preferred_element_type=jnp.float32)
        panel_ref[...] = panel
        ref[pl.ds(at, width), :] = jnp.where(wide < at + width, panel, 0.0)

        def lower_rows(i, carry):
            spot = pl.multiple_of(i * width, width)
            change = lax.dot_general(
                panel_ref[:, pl.ds(spot, width)],
                panel,
                (((0,), (0,)), ((), ())),
                precision=EXACT,
                preferred_element_type=jnp.float32,
            )
            ref[pl.ds(spot, width), :] = jnp.where(inside, 0.0, ref[pl.ds(spot, width), :]) - change
            return carry

        lax.fori_loop(k + 1, n // width, lower_rows, 0)
        return carry

    lax.fori_loop(0, n // width, step, 0)


def factor_whole_kernel(gram_ref, inverse_ref, small_ref, panel_ref, *, scale):
    inverse_ref[...] = gram_ref[...] * scale
    factor_in_place(inverse_ref, small_ref, panel_ref)


def factor_pieces_kernel(place_ref, *refs, scale):
    piece_refs, (inverse_ref, small_ref, panel_ref, held_ref) = refs[:4], refs[4:]
    half = inverse_ref.shape[0] // 2
    rows = half // 2
    for at, piece_ref in enumerate(piece_refs):
        chip, side = place_ref[0] ^ (at // 2), place_ref[1] ^ (at % 2)
        held_ref[chip, pl.ds(pl.multiple_of(side * rows, rows), rows), :] = piece_ref[...] * scale
    inverse_ref[:half, :half] = held_ref[0, :, :half]
    inverse_ref[:half, half : half + rows] = held_ref[0, :, half:]
    inverse_ref[:half, half + rows :] = held_ref[1, :, half:]
    inverse_ref[half:, :half] = jnp.zeros((half, half), jnp.float32)
    inverse_ref[half:, half:] = held_ref[1, :, :half]
    factor_in_place(inverse_ref, small_ref, panel_ref)


def inverse_factor(pieces, place, size, scale):
    width = math.gcd(size, 128)
    vmem = pl.BlockSpec(memory_space=pltpu.VMEM)
    scratch = [pltpu.VMEM((width, width), jnp.float32), pltpu.VMEM((width, size), jnp.float32)]
    if place is None:
        kernel, specs = factor_whole_kernel, [vmem]
    else:
        kernel, specs = factor_pieces_kernel, [pl.BlockSpec(memory_space=pltpu.SMEM)] + [vmem] * 4
        scratch.append(pltpu.VMEM((2, size // 2, size // 4 * 3), jnp.float32))
        pieces = (place, *pieces)
    return pl.pallas_call(
        functools.partial(kernel, scale=scale),
        out_shape=jax.ShapeDtypeStruct((size, size), jnp.float32),
        in_specs=specs,
        out_specs=vmem,
        scratch_shapes=scratch,
        name="inverse_factor",
    )(*pieces)


def standard(genotypes, frequencies):
    spread = lax.rsqrt(2.0 * frequencies * (1.0 - frequencies))
    return ((genotypes.astype(jnp.float32) - 2.0 * frequencies) * spread).astype(jnp.bfloat16)


def unit_columns(matrix):
    return matrix * lax.rsqrt(jnp.mean(matrix * matrix, axis=0, keepdims=True) + 1e-06)


def dot(left_side, right_side, contract, precision):
    return lax.dot_general(
        left_side,
        right_side,
        ((contract[:1], contract[1:]), ((), ())),
        precision=precision,
        preferred_element_type=jnp.float32,
    )


def masks_of(size):
    return [1 << bit for bit in range(size.bit_length() - 1)]


def swap(value, axis, mask):
    size = lax.axis_size(axis)
    return lax.ppermute(value, axis, [(i, i ^ mask) for i in range(size)])


def side_of(axis, mask):
    return jnp.minimum(lax.axis_index(axis) & mask, 1)


def halve(value, axis, mask):
    half = value.shape[0] // 2
    side = side_of(axis, mask)
    kept = lax.dynamic_slice_in_dim(value, side * half, half)
    sent = lax.dynamic_slice_in_dim(value, (1 - side) * half, half)
    return kept + swap(sent, axis, mask)


def double(value, axis, mask):
    side = side_of(axis, mask)
    half = value.shape[0]
    whole = jnp.concatenate([value, value], axis=0)
    return lax.dynamic_update_slice_in_dim(whole, swap(value, axis, mask), (1 - side) * half, 0)


def ring_place(index, size):
    return jnp.where(index % 2 == 0, index // 2, size - (index + 1) // 2)


def ring_member(place, size):
    return jnp.where(2 * place < size, 2 * place, 2 * (size - place) - 1)


def ring_scatter(take, size, forward):
    members = [2 * q if 2 * q < size else 2 * (size - q) - 1 for q in range(size)]
    pairs = [(members[q], members[(q + 1) % size]) for q in range(size)]
    if not forward:
        pairs = [(b, a) for a, b in pairs]
    turn = 1 if forward else -1
    place = ring_place(lax.axis_index("rows"), size)
    total = take(ring_member((place - turn + size) % size, size))
    for step in range(size - 1):
        arrived = lax.ppermute(total, "rows", pairs)
        total = arrived + take(ring_member((place - turn * (step + 2) + 2 * size) % size, size))
    return total


def shares(geno_width, trait_width, rounds):
    tile = math.gcd(math.gcd(geno_width, trait_width), 256) // 2
    geno_half, trait_half = geno_width // 2, trait_width // 2
    first = max((geno_half + trait_half) // rounds // tile * tile - geno_half, tile)
    tiles = (trait_half - first) // tile
    ends = [first + tiles * at // max(rounds - 1, 1) * tile for at in range(rounds)]
    ends[-1] = trait_half
    spans = []
    for at in range(rounds):
        for way in range(2):
            start = ends[at - 1] if at else 0
            geno = (way * geno_half, (way + 1) * geno_half) if at == 0 else (0, 0)
            spans.append((geno, (way * trait_half + start, way * trait_half + ends[at])))
    return spans


def sum_rows(value, masks):
    for mask in masks[:-1]:
        value = halve(value, "rows", mask)
    moved = swap(value, "rows", masks[-1])
    value = value + moved
    for mask in reversed(masks[1:-1]):
        value = double(value, "rows", mask)
    return value


def whole_sum_rows(value, masks):
    moved = swap(value, "rows", masks[0])
    value = value + moved
    for mask in masks[1:-1]:
        value = halve(value, "rows", mask)
    moved = swap(value, "rows", masks[-1])
    value = value + moved
    for mask in reversed(masks[1:-1]):
        value = double(value, "rows", mask)
    return value


def on_device(genotypes, frequencies, traits, geno_sketch, trait_sketch, initial):
    row_count, col_count = lax.axis_size("rows"), lax.axis_size("cols")
    people = genotypes.shape[0] * row_count
    size = geno_sketch.shape[1]
    col = lax.axis_index("cols")
    core, chip = col % 2, col // 2
    chips = col_count // 2
    wide_masks = masks_of(col_count)[1:]
    row_masks = masks_of(row_count)

    standardized = standard(genotypes, frequencies)

    def over_chips(part):
        for mask in wide_masks:
            moved = swap(part, "cols", mask)
            part = part + moved
        return part

    partial_geno = jnp.dot(standardized, geno_sketch, preferred_element_type=jnp.float32)
    chip_geno = halve(partial_geno, "cols", 1)
    height = genotypes.shape[0] // 2
    late_traits, chip_geno = lax.optimization_barrier((traits, chip_geno))
    half_geno = over_chips(chip_geno)
    parts = []
    for at in range(2):
        span = slice(at * (size // 2), (at + 1) * (size // 2))
        part = jnp.dot(late_traits, trait_sketch[:, span], preferred_element_type=jnp.float32)
        chip_part = halve(part, "cols", 1)
        late_traits, chip_part = lax.optimization_barrier((late_traits, chip_part))
        parts.append(over_chips(chip_part))
    half_trait = jnp.concatenate(parts, axis=1)

    mine = jnp.where(core == 0, half_geno, half_trait)
    others = jnp.where(core == 0, half_trait, half_geno)
    arrived = swap(others, "cols", 1)

    def gram_of(left_of, right_of):
        return sum(dot(left_of(view), right_of(view), (0, 0), CLOSE) for view in (mine, arrived))

    def columns(at, width):
        return lambda view: lax.dynamic_slice_in_dim(view, at, width, 1)

    if chips == 2:
        half, quarter = size // 2, size // 4
        block = gram_of(columns(chip * half, half), columns(chip * half, half))
        side = gram_of(columns(0, half), columns(half + chip * quarter, quarter))
        gram = jnp.concatenate([block, side], axis=1)
    else:
        strip = size // chips
        gram = gram_of(columns(chip * strip, strip), lambda view: view)
    mine, others, arrived, gram = lax.optimization_barrier((mine, others, arrived, gram))
    gram = sum_rows(gram, row_masks)

    whole_mine = jnp.concatenate([mine, mine], axis=0)
    own = lax.dynamic_update_slice_in_dim(whole_mine, arrived, (1 - core) * height, 0)
    whole_others = jnp.concatenate([others, others], axis=0)
    other = lax.dynamic_update_slice_in_dim(whole_others, swap(mine, "cols", 1), (1 - core) * height, 0)
    sketch_geno = jnp.where(core == 0, own, other)
    sketch_trait = jnp.where(core == 0, other, own)

    strip = size // col_count
    cross_strip = lax.dynamic_slice_in_dim(sketch_geno, col * strip, strip, 1)
    cross = whole_sum_rows(dot(cross_strip, sketch_trait, (0, 0), CLOSE), row_masks)
    cross = double(cross, "cols", 1)
    for mask in wide_masks:
        cross = double(cross, "cols", mask)

    if chips == 2:
        beside = swap(gram, "rows", 1)
        across = swap(gram, "cols", 2)
        cells = [(r, c) for r in range(row_count) for c in range(col_count)]
        flat = [(r * col_count + c, (r ^ 1) * col_count + (c ^ 2)) for r, c in cells]
        corner = lax.ppermute(gram, ("rows", "cols"), flat)
        place = jnp.stack([chip, side_of("rows", 1)])
        own_inverse = inverse_factor((gram, beside, across, corner), place, size, 1.0 / people)
    else:
        gram = double(gram, "rows", row_masks[0])
        for mask in wide_masks:
            gram = double(gram, "cols", mask)
        own_inverse = inverse_factor((gram,), None, size, 1.0 / people)
    other_inverse = swap(own_inverse, "cols", 1)
    inverse_geno = jnp.where(core == 0, own_inverse, other_inverse)
    inverse_trait = jnp.where(core == 0, other_inverse, own_inverse)

    moved = dot(cross, dot(inverse_trait, initial, (0, 0), CLOSE), (1, 0), CLOSE) / people
    left_dirs = unit_columns(dot(inverse_geno, moved, (1, 0), CLOSE))
    geno_weights = dot(inverse_geno, left_dirs, (0, 0), CLOSE)
    moved = dot(cross, geno_weights, (0, 0), CLOSE) / people
    right_dirs = unit_columns(dot(inverse_trait, moved, (1, 0), CLOSE))
    trait_weights = dot(inverse_trait, right_dirs, (0, 0), CLOSE)

    root_size = math.sqrt(size)
    geno_scores = (dot(sketch_geno, geno_weights, (1, 0), CLOSE) / root_size).astype(jnp.bfloat16)
    trait_scores = (dot(sketch_trait, trait_weights, (1, 0), CLOSE) / root_size).astype(jnp.bfloat16)

    def term(scores, block):
        return lax.dot_general(scores, block, (((0,), (0,)), ((), ())), preferred_element_type=jnp.float32)

    pairs = geno_scores.shape[1]
    share = pairs // row_count
    spans = shares(standardized.shape[1], traits.shape[1], ROUNDS)
    geno_term = term(geno_scores, standardized)
    geno_sums, trait_sums = [], {}
    for at, (geno_span, trait_span) in enumerate(spans):
        trait_term = term(trait_scores, traits[:, slice(*trait_span)])
        edge = geno_span[1] - geno_span[0]
        pieces = [geno_term[:, slice(*geno_span)], trait_term] if edge else [trait_term]

        def take(member, pieces=pieces):
            parts = [lax.dynamic_slice_in_dim(piece, member * share, share) for piece in pieces]
            return jnp.concatenate(parts, axis=1) if len(parts) > 1 else parts[0]

        total = ring_scatter(take, row_count, at % 2 == 0)
        if edge:
            geno_sums.append(total[:, :edge])
        trait_sums[trait_span] = total[:, edge:]
    root_people = math.sqrt(people)
    geno_loadings = jnp.concatenate(geno_sums, axis=1) / root_people
    trait_loadings = jnp.concatenate([trait_sums[span] for span in sorted(trait_sums)], axis=1) / root_people
    return (geno_scores, trait_scores, geno_loadings, trait_loadings)


def solution(mesh):
    placed = (
        P("rows", "cols"),
        P("cols"),
        P("rows", "cols"),
        P("cols", None),
        P("cols", None),
        P(),
    )
    return jax.shard_map(
        on_device,
        mesh=mesh,
        in_specs=placed,
        out_specs=(P("rows", None), P("rows", None), P("rows", "cols"), P("rows", "cols")),
        check_vma=False,
    )
```
